128 devices in a mesh: gy: 8 (over z_lo, y), gz: 16 (over z_hi, x, core).
Axes of the slice: x: 4, y: 4, z: 4 (z_hi: 2, z_lo: 2; z = z_hi * 2 + z_lo), core: 2. Of those that a mesh axis runs over, the one named last changes fastest.
Arguments:
- fixed_volume: bfloat16 [512, 1024, 1024], P(('gy', 'gz')), may hold values from -16 to 16
- moving_volume: bfloat16 [512, 1024, 1024], P(('gy', 'gz')), may hold values from -16 to 16
- displacement: int32 [3, 32, 32], P(None, 'gz', 'gy'), may hold values from -3 to 3
Outputs:
- residual: float32 [256, 512, 512], P('gz', 'gy')
- gradients: float32 [3, 256, 512, 512], P(None, 'gz', 'gy')
The draws below stay inside these ranges and needn't reach their ends.
Inputs may be any that keep to these rules, and one draw needn't show every extreme that they name: Each component of a block's displacement lies within -3 to 3, in coarse voxels; blocks are 8 planes by 16 rows by all 512 columns.
All inputs are finite; a program needn't handle non-finite values.
Results may differ from the reference program's by a relative error of at most 0.005.
Values may be sent and summed in bfloat16 or wider, within the bound.
A program may use at most 128 MiB of HBM per device.

```python
import jax
import jax.numpy as jnp
from jax import lax

NX = 1024
NY = 1024
SHIFT = 3
BZ = 8
BY = 16
NZ = 512
NY2 = 512
NZ2 = 256
RIM = 4


def touch_ends(drawn, own_key, least, high):
    spot = [jax.random.randint(jax.random.fold_in(own_key, axis), (), 0, length) for axis, length in enumerate(drawn.shape)]
    longest = drawn.shape.index(max(drawn.shape))
    neighbour = spot[:longest] + [(spot[longest] + 1) % drawn.shape[longest]] + spot[longest + 1:]
    return drawn.at[tuple(spot)].set(least).at[tuple(neighbour)].set(high)


def level_of(stream_key, dims, split, least, largest):
    level, own = 1.0, jax.random.fold_in(stream_key, 6)
    for dim, shards_of in split:
        heights = jnp.exp(jax.random.uniform(jax.random.fold_in(own, dim), (shards_of,), jnp.float32, least / len(split), largest / len(split)))
        level = level * jnp.repeat(heights, dims[dim] // shards_of).reshape([-1 if axis == dim else 1 for axis in range(len(dims))])
    return level


def normal_values(own_key, dims, deviation, reach, pieces=(), held_as=jnp.bfloat16):
    level = level_of(own_key, dims, pieces, -0.22, 0.18) if pieces else 1.0
    entries = jax.random.normal(own_key, dims, jnp.float32) * deviation * level
    return jnp.minimum(jnp.maximum(entries, -reach), reach).astype(held_as)


def setup_inputs(seed: int = 0) -> dict:
    keys = jax.random.split(jax.random.key(seed), 4)
    return {
        "fixed_volume": normal_values(keys[0], (NZ, NY, NX), 4.0, 16.0, ((0, 128),)),
        "moving_volume": normal_values(keys[1], (NZ, NY, NX), 4.0, 16.0, ((0, 128),)),
        "displacement": touch_ends(jax.random.randint(keys[2], (3, NZ2 // BZ, NY2 // BY), -SHIFT, SHIFT + 1), jax.random.fold_in(keys[2], 1), -SHIFT, SHIFT).astype(jnp.int32),
    }


TAPS = (1.0 / 16.0, 4.0 / 16.0, 6.0 / 16.0, 4.0 / 16.0, 1.0 / 16.0)


def halve_last(values):
    count = values.shape[-1]
    padded = jnp.pad(values, [(0, 0)] * (values.ndim - 1) + [(2, 2)])
    total = jnp.zeros(values.shape[:-1] + (count // 2,), jnp.float32)
    for offset in range(5):
        total = total + TAPS[offset] * padded[..., offset:offset + count:2]
    return total


def plane_level(plane):
    across = halve_last(plane.astype(jnp.float32)).astype(jnp.bfloat16)
    across = lax.optimization_barrier(across).astype(jnp.float32)
    return halve_last(across.T).T.astype(jnp.bfloat16)


def depth_level(rows):
    values = lax.optimization_barrier(rows).astype(jnp.float32)
    return halve_last(values.T).T.astype(jnp.bfloat16)


def pyramid(volume):
    halved = lax.map(plane_level, volume)
    coarse = lax.map(depth_level, halved.transpose(1, 0, 2))
    return coarse.transpose(1, 0, 2)


def warp_row(padded, moves, first_block, row_blocks, width):
    block_rows = jnp.arange(row_blocks, dtype=jnp.int32)
    start_depth = first_block * BZ + RIM - 1 + moves[0]
    start_row = block_rows * BY + RIM - 1 + moves[1]
    start_col = RIM - 1 + moves[2]

    def window(depth_at, row_at, col_at):
        return lax.dynamic_slice(padded, (depth_at, row_at, col_at), (BZ + 2, BY + 2, width + 2))

    windows = jax.vmap(window)(start_depth, start_row, start_col)
    center = windows[:, 1:-1, 1:-1, 1:-1]
    grad_depth = (windows[:, 2:, 1:-1, 1:-1] - windows[:, :-2, 1:-1, 1:-1]) * 0.5
    grad_row = (windows[:, 1:-1, 2:, 1:-1] - windows[:, 1:-1, :-2, 1:-1]) * 0.5
    grad_col = (windows[:, 1:-1, 1:-1, 2:] - windows[:, 1:-1, 1:-1, :-2]) * 0.5
    return jnp.stack([center, grad_depth, grad_row, grad_col])


def reference(fixed_volume, moving_volume, displacement):
    coarse_fixed = pyramid(fixed_volume)
    coarse_moving = pyramid(moving_volume)
    depth_total, row_total, width = coarse_moving.shape
    depth_blocks = depth_total // BZ
    row_blocks = row_total // BY
    padded = jnp.pad(coarse_moving.astype(jnp.float32), RIM)

    def one_row(item):
        first_block, moves = item
        return warp_row(padded, moves, first_block, row_blocks, width)

    stacked = lax.map(one_row, (jnp.arange(depth_blocks, dtype=jnp.int32), displacement.transpose(1, 0, 2)))
    stacked = stacked.transpose(1, 0, 3, 2, 4, 5).reshape(4, depth_total, row_total, width)
    residual = stacked[0] - coarse_fixed.astype(jnp.float32)
    return residual, stacked[1:]
```

```python
import jax
import jax.numpy as jnp
from jax import lax
from jax.experimental import pallas as pl
from jax.experimental.pallas import tpu as pltpu
from jax.sharding import PartitionSpec as P

MESH = pl.DeviceIdType.MESH
BZ = 8
BY = 16
RIM = 4
LAG = 2
GROUP = 8


def decimate_band(fine_count, coarse_count, first):
    rows = lax.broadcasted_iota(jnp.int32, (fine_count, coarse_count), 0)
    columns = lax.broadcasted_iota(jnp.int32, (fine_count, coarse_count), 1)
    offset = rows - 2 * columns + 2 - first
    weight = jnp.where(
        offset == 2,
        6.0,
        jnp.where(
            (offset == 1) | (offset == 3), 4.0, jnp.where((offset == 0) | (offset == 4), 1.0, 0.0)
        ),
    )
    return (weight / 16.0).astype(jnp.bfloat16)


def gray(m):
    return m + m // 2 - 2 * (m // 3)


def pyramid_kernel(
    fixed, moving, bricks, rims,
    fine, band, partial_x, own, up, down, below, above, coarse, relay,
    in_sem, up_send, up_recv, down_send, down_recv,
    first_send, first_recv, second_send, second_recv, rim_send, rim_recv,
):
    gy = lax.axis_index("gy")
    gz = lax.axis_index("gz")
    zlo, y = gy // 4, gy % 4
    zhi, x, lane = gz // 8, (gz // 2) % 4, gz % 8
    place = gy * 16 + gz
    after = (place + 1) % 128
    before = (place + 127) % 128
    rows_fixed = 64
    rows_moving = rows_fixed + 2 * RIM

    loads = []
    for i in range(8):
        for v, volume in enumerate((fixed, moving)):
            copy = pltpu.make_async_copy(
                volume.at[:, pl.ds(128 * i, 128), :],
                fine.at[v, :, pl.ds(16 + 128 * i, 128), :],
                in_sem.at[v, i],
            )
            copy.start()
            loads.append(copy)

    barrier = pltpu.get_barrier_semaphore()

    def greet(to_gy, to_gz):
        pl.semaphore_signal(barrier, inc=1, device_id=(to_gy, to_gz), device_id_type=MESH)

    for k in range(8):
        greet(k, zlo * 8 + lane)
        greet((gz // 8) * 4 + k // 2, (k % 2) * 8 + lane)
        greet(gy, zhi * 8 + k)
    greet(after // 16, after % 16)
    greet(before // 16, before % 16)

    band[0] = decimate_band(640, 256, 0)
    band[1] = decimate_band(640, 256, 128)
    zero_rows = jnp.zeros((2, 4, 16, 1024), jnp.bfloat16)
    fine[:, :, pl.ds(0, 16), :] = zero_rows
    fine[:, :, pl.ds(1040, 16), :] = zero_rows

    @pl.when(place == 0)
    def _():
        below[...] = jnp.zeros_like(below)

    @pl.when(place == 127)
    def _():
        above[...] = jnp.zeros_like(above)

    def up_copy(k):
        return pltpu.make_async_remote_copy(
            up.at[k], below.at[k], up_send.at[k], up_recv.at[k],
            device_id=(after // 16, after % 16), device_id_type=MESH,
        )

    def down_copy(k):
        return pltpu.make_async_remote_copy(
            down.at[k], above.at[k], down_send.at[k], down_recv.at[k],
            device_id=(before // 16, before % 16), device_id_type=MESH,
        )

    def combine(k):
        @pl.when(place > 0)
        def _():
            up_copy(k).wait_recv()

        @pl.when(place < 127)
        def _():
            down_copy(k).wait_recv()

        coarse[k, 0] = (own[k, 0] + below[k].astype(jnp.float32)).astype(jnp.bfloat16)
        coarse[k, 1] = (own[k, 1] + above[k].astype(jnp.float32) * (1.0 / 16.0)).astype(jnp.bfloat16)

    def wait_band(i):
        for v, volume in enumerate((fixed, moving)):
            pltpu.make_async_copy(
                volume.at[:, pl.ds(0, 128), :], fine.at[v, :, pl.ds(16, 128), :], in_sem.at[v, i]
            ).wait()

    wait_band(0)

    def chunk(k, carry):
        @pl.when(k < 7)
        def _():
            wait_band(k + 1)

        for v in range(2):
            taken = fine[v, :, pl.ds(pl.multiple_of(128 * k, 128), 160), :].reshape(640, 1024)
            for half in range(2):
                product = jnp.dot(
                    taken[:, 384 * half:384 * half + 640], band[half],
                    preferred_element_type=jnp.float32,
                )
                product = product.astype(jnp.bfloat16).astype(jnp.float32)
                for q in range(2):
                    partial_x[v, :, 2 * half + q] = product[:, 128 * q:128 * q + 128].reshape(4, 160, 128)
        for v in range(2):
            count = rows_moving if v else rows_fixed
            base = 8 if v else 16
            put = rows_fixed if v else 0
            for q in range(4):
                cols = pl.ds(128 * q, 128)
                half_planes = []
                for p in range(4):
                    tap = [
                        partial_x[v, p, q, pl.ds(base + t - 2, count, stride=2), :] for t in range(5)
                    ]
                    total = (
                        (tap[0] + tap[4]) * 0.0625 + (tap[1] + tap[3]) * 0.25 + tap[2] * 0.375
                    )
                    half_planes.append(total.astype(jnp.bfloat16))
                down[k, pl.ds(put, count), cols] = half_planes[0]
                a0, a1, a2, a3 = [h.astype(jnp.float32) for h in half_planes]
                tail = a2 * 0.0625 + a3 * 0.25
                up[k, pl.ds(put, count), cols] = tail.astype(jnp.bfloat16)
                own[k, 0, pl.ds(put, count), cols] = a0 * 0.375 + a1 * 0.25 + a2 * 0.0625
                own[k, 1, pl.ds(put, count), cols] = (
                    a0 * 0.0625 + a1 * 0.25 + a2 * 0.375 + a3 * 0.25
                )

        @pl.when(k == 0)
        def _():
            pl.semaphore_wait(barrier, 26)

        @pl.when(place < 127)
        def _():
            up_copy(k).start()

        @pl.when(place > 0)
        def _():
            down_copy(k).start()

        @pl.when(k >= LAG)
        def _():
            combine(k - LAG)

        return carry

    lax.fori_loop(0, 8, chunk, 0)
    for k in range(8 - LAG, 8):
        combine(k)

    slot = y * 2 + zhi

    def first_target(i):
        row = (y + gray(i // 2) + 4 - x) % 4
        j = ((i % 2 + zlo) % 2) * 4 + row
        return j, (j == gy) & (zlo == zhi)

    def first_copy(i):
        j, _ = first_target(i)
        return pltpu.make_async_remote_copy(
            coarse.at[j], relay.at[slot], first_send.at[i], first_recv.at[slot],
            device_id=(j, zlo * 8 + lane), device_id_type=MESH,
        )

    def send_first(i, carry):
        j, stays = first_target(i)

        @pl.when(stays)
        def _():
            pltpu.make_async_copy(coarse.at[j], relay.at[slot], first_recv.at[slot]).start()

        @pl.when(jnp.logical_not(stays))
        def _():
            first_copy(i).start()

        return carry

    lax.fori_loop(0, 8, send_first, 0)

    def second_target(i):
        source = (y + 4 - gray(i // 2) + x) % 4
        return source * 2 + i % 2

    def second_copy(i):
        t = second_target(i)
        return pltpu.make_async_remote_copy(
            relay.at[t], bricks.at[lane], second_send.at[i], second_recv.at[lane],
            device_id=(gy, zhi * 8 + t), device_id_type=MESH,
        )

    def send_second(i, carry):
        t = second_target(i)
        pltpu.make_async_copy(coarse.at[0], relay.at[t], first_recv.at[t]).wait()

        @pl.when(t == lane)
        def _():
            pltpu.make_async_copy(relay.at[t], bricks.at[lane], second_recv.at[lane]).start()

        @pl.when(t != lane)
        def _():
            second_copy(i).start()

        return carry

    lax.fori_loop(0, 8, send_second, 0)

    def rim_copy(side, i, s):
        target = gz - 1 if side else gz + 1
        return pltpu.make_async_remote_copy(
            bricks.at[s, :, pl.ds(rows_fixed, rows_moving), :], rims.at[side, i],
            rim_send.at[side, i], rim_recv.at[side, i],
            device_id=(gy, target), device_id_type=MESH,
        )

    def finish(i, carry):
        source = (x + 4 - y + gray(i // 2)) % 4
        s = source * 2 + i % 2
        pltpu.make_async_copy(relay.at[0], bricks.at[s], second_recv.at[s]).wait()

        @pl.when((source == 3) & (gz < 15))
        def _():
            rim_copy(0, i % 2, s).start()

        @pl.when((source == 0) & (gz > 0))
        def _():
            rim_copy(1, i % 2, s).start()

        return carry

    lax.fori_loop(0, 8, finish, 0)

    def drain(k, carry):
        @pl.when(place < 127)
        def _():
            up_copy(k).wait_send()

        @pl.when(place > 0)
        def _():
            down_copy(k).wait_send()

        @pl.when(jnp.logical_not(first_target(k)[1]))
        def _():
            first_copy(k).wait_send()

        @pl.when(second_target(k) != lane)
        def _():
            second_copy(k).wait_send()

        return carry

    lax.fori_loop(0, 8, drain, 0)
    for i in range(2):
        @pl.when(gz < 15)
        def _():
            rim_copy(0, i, 6 + i).wait_send()
            rim_copy(1, i, i).wait_recv()

        @pl.when(gz > 0)
        def _():
            rim_copy(1, i, i).wait_send()
            rim_copy(0, i, 6 + i).wait_recv()


def exchange(fixed_volume, moving_volume):
    bf16 = jnp.bfloat16
    rows = 136
    dma = pltpu.SemaphoreType.DMA
    return pl.pallas_call(
        pyramid_kernel,
        out_shape=[
            jax.ShapeDtypeStruct((8, 2, rows, 512), bf16),
            jax.ShapeDtypeStruct((2, 2, 2, 72, 512), bf16),
        ],
        in_specs=[pl.BlockSpec(memory_space=pl.ANY)] * 2,
        out_specs=[pl.BlockSpec(memory_space=pl.ANY)] * 2,
        scratch_shapes=[
            pltpu.VMEM((2, 4, 1056, 1024), bf16),
            pltpu.VMEM((2, 640, 256), bf16),
            pltpu.VMEM((2, 4, 4, 160, 128), jnp.float32),
            pltpu.VMEM((8, 2, rows, 512), jnp.float32),
            pltpu.VMEM((8, rows, 512), bf16),
            pltpu.VMEM((8, rows, 512), bf16),
            pltpu.VMEM((8, rows, 512), bf16),
            pltpu.VMEM((8, rows, 512), bf16),
            pltpu.VMEM((8, 2, rows, 512), bf16),
            pltpu.VMEM((8, 2, rows, 512), bf16),
            dma((2, 8)),
            dma((8,)), dma((8,)), dma((8,)), dma((8,)),
            dma((8,)), dma((8,)), dma((8,)), dma((8,)),
            dma((2, 2)), dma((2, 2)),
        ],
        compiler_params=pltpu.CompilerParams(
            collective_id=0, has_side_effects=True, vmem_limit_bytes=60 * 2**20
        ),
        name="pyramid",
    )(fixed_volume, moving_volume)


def warp_kernel(moves, bricks, rims, residual, gradients, grid):
    gy = lax.axis_index("gy")
    gz = lax.axis_index("gz")
    block = pl.program_id(0)
    rows = 72

    def put(at, plane):
        for q in range(4):
            grid[at, q] = plane[:, 128 * q:128 * q + 128]

    @pl.when(block == 0)
    def _():
        row = lax.broadcasted_iota(jnp.int32, (rows, 512), 0)
        inside = ((row >= RIM) | (gy > 0)) & ((row < rows - RIM) | (gy < 7))
        for s in range(8):
            for p in range(2):
                plane = bricks[s, p, 64:136, :].astype(jnp.float32)
                put(RIM + 2 * s + p, jnp.where(inside, plane, 0.0))
        for side in range(2):
            there = inside & (gz < 15 if side else gz > 0)
            for i in range(2):
                for p in range(2):
                    plane = rims[side, i, p].astype(jnp.float32)
                    put(side * 20 + 2 * i + p, jnp.where(there, plane, 0.0))

    bz = block // 4
    by = block % 4
    dz = moves[0, bz, by]
    dy = moves[1, bz, by]
    dx = moves[2, bz, by]
    plane0 = bz * BZ + RIM + dz
    row0 = by * BY + RIM + dy
    column = lax.broadcasted_iota(jnp.int32, (BY, 512), 1)

    def shifted(values, by_columns):
        rolled = pltpu.roll(values, (512 - by_columns) % 512, 1)
        at = column + by_columns
        return jnp.where((at >= 0) & (at < 512), rolled, 0.0)

    def window(plane, row):
        return jnp.concatenate([grid[plane, q, pl.ds(row, BY), :] for q in range(4)], axis=1)

    center = [shifted(window(plane0 + i - 1, row0), dx) for i in range(BZ + 2)]
    for i in range(BZ):
        fixed = bricks[4 * bz + i // 2, i % 2, pl.ds(pl.multiple_of(by * BY, BY), BY), :]
        residual[i] = center[i + 1] - fixed.astype(jnp.float32)
        gradients[0, i] = (center[i + 2] - center[i]) * 0.5
        following = window(plane0 + i, row0 + 1)
        preceding = window(plane0 + i, row0 - 1)
        gradients[1, i] = shifted((following - preceding) * 0.5, dx)
        here = window(plane0 + i, row0)
        gradients[2, i] = (shifted(here, dx + 1) - shifted(here, dx - 1)) * 0.5


def warp(displacement, bricks, rims):
    f32 = jnp.float32
    return pl.pallas_call(
        warp_kernel,
        grid=(8,),
        out_shape=[
            jax.ShapeDtypeStruct((16, 64, 512), f32),
            jax.ShapeDtypeStruct((3, 16, 64, 512), f32),
        ],
        in_specs=[
            pl.BlockSpec(memory_space=pltpu.SMEM),
            pl.BlockSpec(memory_space=pltpu.VMEM),
            pl.BlockSpec(memory_space=pltpu.VMEM),
        ],
        out_specs=[
            pl.BlockSpec((BZ, BY, 512), lambda b: (b // 4, b % 4, 0)),
            pl.BlockSpec((3, BZ, BY, 512), lambda b: (0, b // 4, b % 4, 0)),
        ],
        scratch_shapes=[pltpu.VMEM((24, 4, 72, 128), f32)],
        name="warp",
    )(displacement, bricks, rims)


def shards(fixed_volume, moving_volume, displacement):
    bricks, rims = exchange(fixed_volume, moving_volume)
    residual, gradients = warp(displacement, bricks, rims)
    return residual, gradients


def solution(mesh):
    placed = (P(("gy", "gz"), None, None), P(("gy", "gz"), None, None), P(None, "gz", "gy"))
    return jax.shard_map(
        shards,
        mesh=mesh,
        in_specs=placed,
        out_specs=(P("gz", "gy", None), P(None, "gz", "gy", None)),
        check_vma=False,
    )
```

```python
import jax
import jax.numpy as jnp
from jax import lax
from jax.experimental import pallas as pl
from jax.experimental.pallas import tpu as pltpu
from jax.sharding import PartitionSpec as P

MESH = pl.DeviceIdType.MESH
BZ = 8
BY = 16
RIM = 4
LAG = 2
RELAY_LAG = 4


def decimate_band(fine_count, coarse_count, first):
    rows = lax.broadcasted_iota(jnp.int32, (fine_count, coarse_count), 0)
    columns = lax.broadcasted_iota(jnp.int32, (fine_count, coarse_count), 1)
    offset = rows - 2 * columns + 2 - first
    weight = jnp.where(
        offset == 2,
        6.0,
        jnp.where(
            (offset == 1) | (offset == 3), 4.0, jnp.where((offset == 0) | (offset == 4), 1.0, 0.0)
        ),
    )
    return (weight / 16.0).astype(jnp.bfloat16)


def gray(m):
    return m + m // 2 - 2 * (m // 3)


def pyramid_kernel(
    fixed, moving, bricks, rims,
    fine, band, partial_x, own, up, down, below, above, coarse, column, relay,
    in_sem, up_send, up_recv, down_send, down_recv,
    row_send, row_recv, depth_send, depth_recv, second_send, second_recv, rim_send, rim_recv,
):
    gy = lax.axis_index("gy")
    gz = lax.axis_index("gz")
    zlo, y = gy // 4, gy % 4
    zhi, x, lane = gz // 8, (gz // 2) % 4, gz % 8
    place = gy * 16 + gz
    after = (place + 1) % 128
    before = (place + 127) % 128
    rows_fixed = 64
    rows_moving = rows_fixed + 2 * RIM

    loads = []
    for i in range(8):
        for v, volume in enumerate((fixed, moving)):
            copy = pltpu.make_async_copy(
                volume.at[:, pl.ds(128 * i, 128), :],
                fine.at[v, :, pl.ds(16 + 128 * i, 128), :],
                in_sem.at[v, i],
            )
            copy.start()
            loads.append(copy)

    barrier = pltpu.get_barrier_semaphore()

    def greet(to_gy, to_gz):
        pl.semaphore_signal(barrier, inc=1, device_id=(to_gy, to_gz), device_id_type=MESH)

    for k in range(8):
        greet(gy, zhi * 8 + k)
    for k in range(4):
        greet(zlo * 4 + k, gz)
    for k in range(2):
        greet(k * 4 + y, zlo * 8 + lane)
        greet(zhi * 4 + y, k * 8 + lane)
    greet(after // 16, after % 16)
    greet(before // 16, before % 16)

    band[0] = decimate_band(640, 256, 0)
    band[1] = decimate_band(640, 256, 128)
    zero_rows = jnp.zeros((2, 4, 16, 1024), jnp.bfloat16)
    fine[:, :, pl.ds(0, 16), :] = zero_rows
    fine[:, :, pl.ds(1040, 16), :] = zero_rows

    @pl.when(place == 0)
    def _():
        below[...] = jnp.zeros_like(below)

    @pl.when(place == 127)
    def _():
        above[...] = jnp.zeros_like(above)

    def up_copy(k):
        return pltpu.make_async_remote_copy(
            up.at[k], below.at[k], up_send.at[k], up_recv.at[k],
            device_id=(after // 16, after % 16), device_id_type=MESH,
        )

    def down_copy(k):
        return pltpu.make_async_remote_copy(
            down.at[k], above.at[k], down_send.at[k], down_recv.at[k],
            device_id=(before // 16, before % 16), device_id_type=MESH,
        )

    def combine(k):
        @pl.when(place > 0)
        def _():
            up_copy(k).wait_recv()

        @pl.when(place < 127)
        def _():
            down_copy(k).wait_recv()

        coarse[k, 0] = (own[k, 0] + below[k].astype(jnp.float32)).astype(jnp.bfloat16)
        coarse[k, 1] = (own[k, 1] + above[k].astype(jnp.float32) * (1.0 / 16.0)).astype(jnp.bfloat16)

    def wait_band(i):
        for v, volume in enumerate((fixed, moving)):
            pltpu.make_async_copy(
                volume.at[:, pl.ds(0, 128), :], fine.at[v, :, pl.ds(16, 128), :], in_sem.at[v, i]
            ).wait()

    wait_band(0)

    def chunk(k, carry):
        @pl.when(k < 7)
        def _():
            wait_band(k + 1)

        for v in range(2):
            taken = fine[v, :, pl.ds(pl.multiple_of(128 * k, 128), 160), :].reshape(640, 1024)
            for half in range(2):
                product = jnp.dot(
                    taken[:, 384 * half:384 * half + 640], band[half],
                    preferred_element_type=jnp.float32,
                )
                product = product.astype(jnp.bfloat16).astype(jnp.float32)
                for q in range(2):
                    partial_x[v, :, 2 * half + q] = product[:, 128 * q:128 * q + 128].reshape(4, 160, 128)
        for v in range(2):
            count = rows_moving if v else rows_fixed
            base = 8 if v else 16
            put = rows_fixed if v else 0
            for q in range(4):
                cols = pl.ds(128 * q, 128)
                half_planes = []
                for p in range(4):
                    tap = [
                        partial_x[v, p, q, pl.ds(base + t - 2, count, stride=2), :] for t in range(5)
                    ]
                    total = (
                        (tap[0] + tap[4]) * 0.0625 + (tap[1] + tap[3]) * 0.25 + tap[2] * 0.375
                    )
                    half_planes.append(total.astype(jnp.bfloat16))
                down[k, pl.ds(put, count), cols] = half_planes[0]
                a0, a1, a2, a3 = [h.astype(jnp.float32) for h in half_planes]
                tail = a2 * 0.0625 + a3 * 0.25
                up[k, pl.ds(put, count), cols] = tail.astype(jnp.bfloat16)
                own[k, 0, pl.ds(put, count), cols] = a0 * 0.375 + a1 * 0.25 + a2 * 0.0625
                own[k, 1, pl.ds(put, count), cols] = (
                    a0 * 0.0625 + a1 * 0.25 + a2 * 0.375 + a3 * 0.25
                )

        @pl.when(k == 0)
        def _():
            pl.semaphore_wait(barrier, 18)

        @pl.when(place < 127)
        def _():
            up_copy(k).start()

        @pl.when(place > 0)
        def _():
            down_copy(k).start()

        @pl.when(k >= LAG)
        def _():
            combine(k - LAG)

        return carry

    lax.fori_loop(0, 8, chunk, 0)
    for k in range(8 - LAG, 8):
        combine(k)

    def row_target(i):
        return (y + gray(i // 2) + 4 - x) % 4, (i % 2 + zlo) % 2

    def row_copy(i):
        row, part = row_target(i)
        return pltpu.make_async_remote_copy(
            coarse.at[part * 4 + row], column.at[y * 2 + part],
            row_send.at[i], row_recv.at[y * 2 + part],
            device_id=(zlo * 4 + row, gz), device_id_type=MESH,
        )

    def send_row(i, carry):
        row, part = row_target(i)

        @pl.when(row == y)
        def _():
            pltpu.make_async_copy(
                coarse.at[part * 4 + row], column.at[y * 2 + part], row_recv.at[y * 2 + part]
            ).start()

        @pl.when(row != y)
        def _():
            row_copy(i).start()

        return carry

    lax.fori_loop(0, 8, send_row, 0)

    def depth_target(i):
        source = (y + 4 - gray(i // 2) + x) % 4
        part = (i % 2 + zlo) % 2
        return source, part, (part == zlo) & (zlo == zhi)

    def depth_copy(i):
        source, part, _ = depth_target(i)
        return pltpu.make_async_remote_copy(
            column.at[source * 2 + part], relay.at[source * 2 + zhi],
            depth_send.at[i], depth_recv.at[source * 2 + zhi],
            device_id=(part * 4 + y, zlo * 8 + lane), device_id_type=MESH,
        )

    def send_depth(i):
        source, part, stays = depth_target(i)
        slot = source * 2 + part
        pltpu.make_async_copy(coarse.at[0], column.at[slot], row_recv.at[slot]).wait()

        @pl.when(stays)
        def _():
            pltpu.make_async_copy(
                column.at[slot], relay.at[source * 2 + zhi], depth_recv.at[source * 2 + zhi]
            ).start()

        @pl.when(jnp.logical_not(stays))
        def _():
            depth_copy(i).start()

    def second_target(i):
        source = (y + 4 - gray(i // 2) + x) % 4
        return source * 2 + i % 2

    def second_copy(i):
        t = second_target(i)
        return pltpu.make_async_remote_copy(
            relay.at[t], bricks.at[lane], second_send.at[i], second_recv.at[lane],
            device_id=(gy, zhi * 8 + t), device_id_type=MESH,
        )

    def send_second(i):
        t = second_target(i)
        pltpu.make_async_copy(column.at[0], relay.at[t], depth_recv.at[t]).wait()

        @pl.when(t == lane)
        def _():
            pltpu.make_async_copy(relay.at[t], bricks.at[lane], second_recv.at[lane]).start()

        @pl.when(t != lane)
        def _():
            second_copy(i).start()

    def pass_on(i, carry):
        @pl.when(i < 8)
        def _():
            send_depth(i)

        @pl.when(i >= RELAY_LAG)
        def _():
            send_second(i - RELAY_LAG)

        return carry

    lax.fori_loop(0, 8 + RELAY_LAG, pass_on, 0)

    def rim_copy(side, i, s):
        target = gz - 1 if side else gz + 1
        return pltpu.make_async_remote_copy(
            bricks.at[s, :, pl.ds(rows_fixed, rows_moving), :], rims.at[side, i],
            rim_send.at[side, i], rim_recv.at[side, i],
            device_id=(gy, target), device_id_type=MESH,
        )

    def finish(i, carry):
        source = (x + 4 - y + gray(i // 2)) % 4
        s = source * 2 + i % 2
        pltpu.make_async_copy(relay.at[0], bricks.at[s], second_recv.at[s]).wait()

        @pl.when((source == 3) & (gz < 15))
        def _():
            rim_copy(0, i % 2, s).start()

        @pl.when((source == 0) & (gz > 0))
        def _():
            rim_copy(1, i % 2, s).start()

        return carry

    lax.fori_loop(0, 8, finish, 0)

    def drain(k, carry):
        @pl.when(place < 127)
        def _():
            up_copy(k).wait_send()

        @pl.when(place > 0)
        def _():
            down_copy(k).wait_send()

        @pl.when(row_target(k)[0] != y)
        def _():
            row_copy(k).wait_send()

        @pl.when(jnp.logical_not(depth_target(k)[2]))
        def _():
            depth_copy(k).wait_send()

        @pl.when(second_target(k) != lane)
        def _():
            second_copy(k).wait_send()

        return carry

    lax.fori_loop(0, 8, drain, 0)
    for i in range(2):
        @pl.when(gz < 15)
        def _():
            rim_copy(0, i, 6 + i).wait_send()
            rim_copy(1, i, i).wait_recv()

        @pl.when(gz > 0)
        def _():
            rim_copy(1, i, i).wait_send()
            rim_copy(0, i, 6 + i).wait_recv()


def exchange(fixed_volume, moving_volume):
    bf16 = jnp.bfloat16
    rows = 136
    dma = pltpu.SemaphoreType.DMA
    return pl.pallas_call(
        pyramid_kernel,
        out_shape=[
            jax.ShapeDtypeStruct((8, 2, rows, 512), bf16),
            jax.ShapeDtypeStruct((2, 2, 2, 72, 512), bf16),
        ],
        in_specs=[pl.BlockSpec(memory_space=pl.ANY)] * 2,
        out_specs=[pl.BlockSpec(memory_space=pl.ANY)] * 2,
        scratch_shapes=[
            pltpu.VMEM((2, 4, 1056, 1024), bf16),
            pltpu.VMEM((2, 640, 256), bf16),
            pltpu.VMEM((2, 4, 4, 160, 128), jnp.float32),
            pltpu.VMEM((8, 2, rows, 512), jnp.float32),
            pltpu.VMEM((8, rows, 512), bf16),
            pltpu.VMEM((8, rows, 512), bf16),
            pltpu.VMEM((8, rows, 512), bf16),
            pltpu.VMEM((8, rows, 512), bf16),
            pltpu.VMEM((8, 2, rows, 512), bf16),
            pltpu.VMEM((8, 2, rows, 512), bf16),
            pltpu.VMEM((8, 2, rows, 512), bf16),
            dma((2, 8)),
            dma((8,)), dma((8,)), dma((8,)), dma((8,)),
            dma((8,)), dma((8,)), dma((8,)), dma((8,)), dma((8,)), dma((8,)),
            dma((2, 2)), dma((2, 2)),
        ],
        compiler_params=pltpu.CompilerParams(
            collective_id=0, has_side_effects=True, vmem_limit_bytes=60 * 2**20
        ),
        name="pyramid",
    )(fixed_volume, moving_volume)


def warp_kernel(moves, bricks, rims, residual, gradients, grid):
    gy = lax.axis_index("gy")
    gz = lax.axis_index("gz")
    block = pl.program_id(0)
    rows = 72

    def put(at, plane):
        for q in range(4):
            grid[at, q] = plane[:, 128 * q:128 * q + 128]

    @pl.when(block == 0)
    def _():
        row = lax.broadcasted_iota(jnp.int32, (rows, 512), 0)
        inside = ((row >= RIM) | (gy > 0)) & ((row < rows - RIM) | (gy < 7))
        for s in range(8):
            for p in range(2):
                plane = bricks[s, p, 64:136, :].astype(jnp.float32)
                put(RIM + 2 * s + p, jnp.where(inside, plane, 0.0))
        for side in range(2):
            there = inside & (gz < 15 if side else gz > 0)
            for i in range(2):
                for p in range(2):
                    plane = rims[side, i, p].astype(jnp.float32)
                    put(side * 20 + 2 * i + p, jnp.where(there, plane, 0.0))

    bz = block // 4
    by = block % 4
    dz = moves[0, bz, by]
    dy = moves[1, bz, by]
    dx = moves[2, bz, by]
    plane0 = bz * BZ + RIM + dz
    row0 = by * BY + RIM + dy
    column = lax.broadcasted_iota(jnp.int32, (BY, 512), 1)

    def shifted(values, by_columns):
        rolled = pltpu.roll(values, (512 - by_columns) % 512, 1)
        at = column + by_columns
        return jnp.where((at >= 0) & (at < 512), rolled, 0.0)

    def window(plane, row):
        return jnp.concatenate([grid[plane, q, pl.ds(row, BY), :] for q in range(4)], axis=1)

    center = [shifted(window(plane0 + i - 1, row0), dx) for i in range(BZ + 2)]
    for i in range(BZ):
        fixed = bricks[4 * bz + i // 2, i % 2, pl.ds(pl.multiple_of(by * BY, BY), BY), :]
        residual[i] = center[i + 1] - fixed.astype(jnp.float32)
        gradients[0, i] = (center[i + 2] - center[i]) * 0.5
        following = window(plane0 + i, row0 + 1)
        preceding = window(plane0 + i, row0 - 1)
        gradients[1, i] = shifted((following - preceding) * 0.5, dx)
        here = window(plane0 + i, row0)
        gradients[2, i] = (shifted(here, dx + 1) - shifted(here, dx - 1)) * 0.5


def warp(displacement, bricks, rims):
    f32 = jnp.float32
    return pl.pallas_call(
        warp_kernel,
        grid=(8,),
        out_shape=[
            jax.ShapeDtypeStruct((16, 64, 512), f32),
            jax.ShapeDtypeStruct((3, 16, 64, 512), f32),
        ],
        in_specs=[
            pl.BlockSpec(memory_space=pltpu.SMEM),
            pl.BlockSpec(memory_space=pltpu.VMEM),
            pl.BlockSpec(memory_space=pltpu.VMEM),
        ],
        out_specs=[
            pl.BlockSpec((BZ, BY, 512), lambda b: (b // 4, b % 4, 0)),
            pl.BlockSpec((3, BZ, BY, 512), lambda b: (0, b // 4, b % 4, 0)),
        ],
        scratch_shapes=[pltpu.VMEM((24, 4, 72, 128), f32)],
        name="warp",
    )(displacement, bricks, rims)


def shards(fixed_volume, moving_volume, displacement):
    bricks, rims = exchange(fixed_volume, moving_volume)
    residual, gradients = warp(displacement, bricks, rims)
    return residual, gradients


def solution(mesh):
    placed = (P(("gy", "gz"), None, None), P(("gy", "gz"), None, None), P(None, "gz", "gy"))
    return jax.shard_map(
        shards,
        mesh=mesh,
        in_specs=placed,
        out_specs=(P("gz", "gy", None), P(None, "gz", "gy", None)),
        check_vma=False,
    )
```

```python
import jax
import jax.numpy as jnp
from jax import lax
from jax.experimental import pallas as pl
from jax.experimental.pallas import tpu as pltpu
from jax.sharding import PartitionSpec as P

MESH = pl.DeviceIdType.MESH
BZ = 8
BY = 16
RIM = 4
LAG = 2
RELAY_LAG = 4


def decimate_band(fine_count, coarse_count, first):
    rows = lax.broadcasted_iota(jnp.int32, (fine_count, coarse_count), 0)
    columns = lax.broadcasted_iota(jnp.int32, (fine_count, coarse_count), 1)
    offset = rows - 2 * columns + 2 - first
    weight = jnp.where(
        offset == 2,
        6.0,
        jnp.where(
            (offset == 1) | (offset == 3), 4.0, jnp.where((offset == 0) | (offset == 4), 1.0, 0.0)
        ),
    )
    return (weight / 16.0).astype(jnp.bfloat16)


def gray(m):
    return m + m // 2 - 2 * (m // 3)


def pyramid_kernel(
    fixed, moving, bricks, rims,
    fine, band, partial_x, own, up, down, below, above, coarse, column, relay,
    in_sem, up_send, up_recv, down_send, down_recv,
    row_send, row_recv, depth_send, depth_recv, second_send, second_recv, rim_send, rim_recv,
):
    gy = lax.axis_index("gy")
    gz = lax.axis_index("gz")
    zlo, y = gy // 4, gy % 4
    zhi, x, lane = gz // 8, (gz // 2) % 4, gz % 8
    place = gy * 16 + gz
    after = (place + 1) % 128
    before = (place + 127) % 128
    rows_fixed = 64
    rows_moving = rows_fixed + 2 * RIM

    loads = []
    for i in range(8):
        for v, volume in enumerate((fixed, moving)):
            copy = pltpu.make_async_copy(
                volume.at[:, pl.ds(128 * i, 128), :],
                fine.at[v, :, pl.ds(16 + 128 * i, 128), :],
                in_sem.at[v, i],
            )
            copy.start()
            loads.append(copy)

    barrier = pltpu.get_barrier_semaphore()

    def greet(to_gy, to_gz):
        pl.semaphore_signal(barrier, inc=1, device_id=(to_gy, to_gz), device_id_type=MESH)

    for k in range(8):
        greet(gy, zhi * 8 + k)
    for k in range(4):
        greet(zlo * 4 + k, gz)
    for k in range(2):
        greet(k * 4 + y, zlo * 8 + lane)
        greet(zhi * 4 + y, k * 8 + lane)
    greet(after // 16, after % 16)
    greet(before // 16, before % 16)

    band[0] = decimate_band(640, 256, 0)
    band[1] = decimate_band(640, 256, 128)
    zero_rows = jnp.zeros((2, 4, 16, 1024), jnp.bfloat16)
    fine[:, :, pl.ds(0, 16), :] = zero_rows
    fine[:, :, pl.ds(1040, 16), :] = zero_rows

    @pl.when(place == 0)
    def _():
        below[...] = jnp.zeros_like(below)

    @pl.when(place == 127)
    def _():
        above[...] = jnp.zeros_like(above)

    def up_copy(k):
        return pltpu.make_async_remote_copy(
            up.at[k], below.at[k], up_send.at[k], up_recv.at[k],
            device_id=(after // 16, after % 16), device_id_type=MESH,
        )

    def down_copy(k):
        return pltpu.make_async_remote_copy(
            down.at[k], above.at[k], down_send.at[k], down_recv.at[k],
            device_id=(before // 16, before % 16), device_id_type=MESH,
        )

    def combine(k):
        @pl.when(place > 0)
        def _():
            up_copy(k).wait_recv()

        @pl.when(place < 127)
        def _():
            down_copy(k).wait_recv()

        coarse[k, 0] = (own[k, 0] + below[k].astype(jnp.float32)).astype(jnp.bfloat16)
        coarse[k, 1] = (own[k, 1] + above[k].astype(jnp.float32) * (1.0 / 16.0)).astype(jnp.bfloat16)

    def wait_band(i):
        for v, volume in enumerate((fixed, moving)):
            pltpu.make_async_copy(
                volume.at[:, pl.ds(0, 128), :], fine.at[v, :, pl.ds(16, 128), :], in_sem.at[v, i]
            ).wait()

    wait_band(0)

    def chunk(k, carry):
        @pl.when(k < 7)
        def _():
            wait_band(k + 1)

        for v in range(2):
            taken = fine[v, :, pl.ds(pl.multiple_of(128 * k, 128), 160), :].reshape(640, 1024)
            for half in range(2):
                product = jnp.dot(
                    taken[:, 384 * half:384 * half + 640], band[half],
                    preferred_element_type=jnp.float32,
                )
                product = product.astype(jnp.bfloat16).astype(jnp.float32)
                for q in range(2):
                    partial_x[v, :, 2 * half + q] = product[:, 128 * q:128 * q + 128].reshape(4, 160, 128)
        for v in range(2):
            count = rows_moving if v else rows_fixed
            base = 8 if v else 16
            put = rows_fixed if v else 0
            for q in range(4):
                cols = pl.ds(128 * q, 128)
                half_planes = []
                for p in range(4):
                    tap = [
                        partial_x[v, p, q, pl.ds(base + t - 2, count, stride=2), :] for t in range(5)
                    ]
                    total = (
                        (tap[0] + tap[4]) * 0.0625 + (tap[1] + tap[3]) * 0.25 + tap[2] * 0.375
                    )
                    half_planes.append(total.astype(jnp.bfloat16))
                down[k, pl.ds(put, count), cols] = half_planes[0]
                a0, a1, a2, a3 = [h.astype(jnp.float32) for h in half_planes]
                tail = a2 * 0.0625 + a3 * 0.25
                up[k, pl.ds(put, count), cols] = tail.astype(jnp.bfloat16)
                own[k, 0, pl.ds(put, count), cols] = a0 * 0.375 + a1 * 0.25 + a2 * 0.0625
                own[k, 1, pl.ds(put, count), cols] = (
                    a0 * 0.0625 + a1 * 0.25 + a2 * 0.375 + a3 * 0.25
                )

        @pl.when(k == 0)
        def _():
            pl.semaphore_wait(barrier, 18)

        @pl.when(place < 127)
        def _():
            up_copy(k).start()

        @pl.when(place > 0)
        def _():
            down_copy(k).start()

        @pl.when(k >= LAG)
        def _():
            combine(k - LAG)

        return carry

    lax.fori_loop(0, 8, chunk, 0)
    for k in range(8 - LAG, 8):
        combine(k)

    def row_target(i):
        return (y + gray(i // 2)) % 4, (i % 2 + zlo) % 2

    def row_copy(i):
        row, part = row_target(i)
        return pltpu.make_async_remote_copy(
            coarse.at[part * 4 + row], column.at[y * 2 + part],
            row_send.at[i], row_recv.at[y * 2 + part],
            device_id=(zlo * 4 + row, gz), device_id_type=MESH,
        )

    def send_row(i, carry):
        row, part = row_target(i)

        @pl.when(row == y)
        def _():
            pltpu.make_async_copy(
                coarse.at[part * 4 + row], column.at[y * 2 + part], row_recv.at[y * 2 + part]
            ).start()

        @pl.when(row != y)
        def _():
            row_copy(i).start()

        return carry

    lax.fori_loop(0, 8, send_row, 0)

    def depth_target(i):
        source = (y + 4 - gray(i // 2)) % 4
        part = (i % 2 + zlo) % 2
        return source, part, (part == zlo) & (zlo == zhi)

    def depth_copy(i):
        source, part, _ = depth_target(i)
        return pltpu.make_async_remote_copy(
            column.at[source * 2 + part], relay.at[source * 2 + zhi],
            depth_send.at[i], depth_recv.at[source * 2 + zhi],
            device_id=(part * 4 + y, zlo * 8 + lane), device_id_type=MESH,
        )

    def send_depth(i):
        source, part, stays = depth_target(i)
        slot = source * 2 + part
        pltpu.make_async_copy(coarse.at[0], column.at[slot], row_recv.at[slot]).wait()

        @pl.when(stays)
        def _():
            pltpu.make_async_copy(
                column.at[slot], relay.at[source * 2 + zhi], depth_recv.at[source * 2 + zhi]
            ).start()

        @pl.when(jnp.logical_not(stays))
        def _():
            depth_copy(i).start()

    def second_target(i):
        source = (y + 4 - gray(i // 2)) % 4
        return source * 2 + i % 2

    def second_copy(i):
        t = second_target(i)
        return pltpu.make_async_remote_copy(
            relay.at[t], bricks.at[lane], second_send.at[i], second_recv.at[lane],
            device_id=(gy, zhi * 8 + t), device_id_type=MESH,
        )

    def send_second(i):
        t = second_target(i)
        pltpu.make_async_copy(column.at[0], relay.at[t], depth_recv.at[t]).wait()

        @pl.when(t == lane)
        def _():
            pltpu.make_async_copy(relay.at[t], bricks.at[lane], second_recv.at[lane]).start()

        @pl.when(t != lane)
        def _():
            second_copy(i).start()

    def pass_on(i, carry):
        @pl.when(i < 8)
        def _():
            send_depth(i)

        @pl.when(i >= RELAY_LAG)
        def _():
            send_second(i - RELAY_LAG)

        return carry

    lax.fori_loop(0, 8 + RELAY_LAG, pass_on, 0)

    def rim_copy(side, i, s):
        target = gz - 1 if side else gz + 1
        return pltpu.make_async_remote_copy(
            bricks.at[s, :, pl.ds(rows_fixed, rows_moving), :], rims.at[side, i],
            rim_send.at[side, i], rim_recv.at[side, i],
            device_id=(gy, target), device_id_type=MESH,
        )

    def finish(i, carry):
        source = (x + 4 - y + gray(i // 2)) % 4
        s = source * 2 + i % 2
        pltpu.make_async_copy(relay.at[0], bricks.at[s], second_recv.at[s]).wait()

        @pl.when((source == 3) & (gz < 15))
        def _():
            rim_copy(0, i % 2, s).start()

        @pl.when((source == 0) & (gz > 0))
        def _():
            rim_copy(1, i % 2, s).start()

        return carry

    lax.fori_loop(0, 8, finish, 0)

    def drain(k, carry):
        @pl.when(place < 127)
        def _():
            up_copy(k).wait_send()

        @pl.when(place > 0)
        def _():
            down_copy(k).wait_send()

        @pl.when(row_target(k)[0] != y)
        def _():
            row_copy(k).wait_send()

        @pl.when(jnp.logical_not(depth_target(k)[2]))
        def _():
            depth_copy(k).wait_send()

        @pl.when(second_target(k) != lane)
        def _():
            second_copy(k).wait_send()

        return carry

    lax.fori_loop(0, 8, drain, 0)
    for i in range(2):
        @pl.when(gz < 15)
        def _():
            rim_copy(0, i, 6 + i).wait_send()
            rim_copy(1, i, i).wait_recv()

        @pl.when(gz > 0)
        def _():
            rim_copy(1, i, i).wait_send()
            rim_copy(0, i, 6 + i).wait_recv()


def exchange(fixed_volume, moving_volume):
    bf16 = jnp.bfloat16
    rows = 136
    dma = pltpu.SemaphoreType.DMA
    return pl.pallas_call(
        pyramid_kernel,
        out_shape=[
            jax.ShapeDtypeStruct((8, 2, rows, 512), bf16),
            jax.ShapeDtypeStruct((2, 2, 2, 72, 512), bf16),
        ],
        in_specs=[pl.BlockSpec(memory_space=pl.ANY)] * 2,
        out_specs=[pl.BlockSpec(memory_space=pl.ANY)] * 2,
        scratch_shapes=[
            pltpu.VMEM((2, 4, 1056, 1024), bf16),
            pltpu.VMEM((2, 640, 256), bf16),
            pltpu.VMEM((2, 4, 4, 160, 128), jnp.float32),
            pltpu.VMEM((8, 2, rows, 512), jnp.float32),
            pltpu.VMEM((8, rows, 512), bf16),
            pltpu.VMEM((8, rows, 512), bf16),
            pltpu.VMEM((8, rows, 512), bf16),
            pltpu.VMEM((8, rows, 512), bf16),
            pltpu.VMEM((8, 2, rows, 512), bf16),
            pltpu.VMEM((8, 2, rows, 512), bf16),
            pltpu.VMEM((8, 2, rows, 512), bf16),
            dma((2, 8)),
            dma((8,)), dma((8,)), dma((8,)), dma((8,)),
            dma((8,)), dma((8,)), dma((8,)), dma((8,)), dma((8,)), dma((8,)),
            dma((2, 2)), dma((2, 2)),
        ],
        compiler_params=pltpu.CompilerParams(
            collective_id=0, has_side_effects=True, vmem_limit_bytes=60 * 2**20
        ),
        name="pyramid",
    )(fixed_volume, moving_volume)


def warp_kernel(moves, bricks, rims, residual, gradients, grid):
    gy = lax.axis_index("gy")
    gz = lax.axis_index("gz")
    block = pl.program_id(0)
    rows = 72

    def put(at, plane):
        for q in range(4):
            grid[at, q] = plane[:, 128 * q:128 * q + 128]

    @pl.when(block == 0)
    def _():
        row = lax.broadcasted_iota(jnp.int32, (rows, 512), 0)
        inside = ((row >= RIM) | (gy > 0)) & ((row < rows - RIM) | (gy < 7))
        for s in range(8):
            for p in range(2):
                plane = bricks[s, p, 64:136, :].astype(jnp.float32)
                put(RIM + 2 * s + p, jnp.where(inside, plane, 0.0))
        for side in range(2):
            there = inside & (gz < 15 if side else gz > 0)
            for i in range(2):
                for p in range(2):
                    plane = rims[side, i, p].astype(jnp.float32)
                    put(side * 20 + 2 * i + p, jnp.where(there, plane, 0.0))

    bz = block // 4
    by = block % 4
    dz = moves[0, bz, by]
    dy = moves[1, bz, by]
    dx = moves[2, bz, by]
    plane0 = bz * BZ + RIM + dz
    row0 = by * BY + RIM + dy
    column = lax.broadcasted_iota(jnp.int32, (BY, 512), 1)

    def shifted(values, by_columns):
        rolled = pltpu.roll(values, (512 - by_columns) % 512, 1)
        at = column + by_columns
        return jnp.where((at >= 0) & (at < 512), rolled, 0.0)

    def window(plane, row):
        return jnp.concatenate([grid[plane, q, pl.ds(row, BY), :] for q in range(4)], axis=1)

    center = [shifted(window(plane0 + i - 1, row0), dx) for i in range(BZ + 2)]
    for i in range(BZ):
        fixed = bricks[4 * bz + i // 2, i % 2, pl.ds(pl.multiple_of(by * BY, BY), BY), :]
        residual[i] = center[i + 1] - fixed.astype(jnp.float32)
        gradients[0, i] = (center[i + 2] - center[i]) * 0.5
        following = window(plane0 + i, row0 + 1)
        preceding = window(plane0 + i, row0 - 1)
        gradients[1, i] = shifted((following - preceding) * 0.5, dx)
        here = window(plane0 + i, row0)
        gradients[2, i] = (shifted(here, dx + 1) - shifted(here, dx - 1)) * 0.5


def warp(displacement, bricks, rims):
    f32 = jnp.float32
    return pl.pallas_call(
        warp_kernel,
        grid=(8,),
        out_shape=[
            jax.ShapeDtypeStruct((16, 64, 512), f32),
            jax.ShapeDtypeStruct((3, 16, 64, 512), f32),
        ],
        in_specs=[
            pl.BlockSpec(memory_space=pltpu.SMEM),
            pl.BlockSpec(memory_space=pltpu.VMEM),
            pl.BlockSpec(memory_space=pltpu.VMEM),
        ],
        out_specs=[
            pl.BlockSpec((BZ, BY, 512), lambda b: (b // 4, b % 4, 0)),
            pl.BlockSpec((3, BZ, BY, 512), lambda b: (0, b // 4, b % 4, 0)),
        ],
        scratch_shapes=[pltpu.VMEM((24, 4, 72, 128), f32)],
        name="warp",
    )(displacement, bricks, rims)


def shards(fixed_volume, moving_volume, displacement):
    bricks, rims = exchange(fixed_volume, moving_volume)
    residual, gradients = warp(displacement, bricks, rims)
    return residual, gradients


def solution(mesh):
    placed = (P(("gy", "gz"), None, None), P(("gy", "gz"), None, None), P(None, "gz", "gy"))
    return jax.shard_map(
        shards,
        mesh=mesh,
        in_specs=placed,
        out_specs=(P("gz", "gy", None), P(None, "gz", "gy", None)),
        check_vma=False,
    )
```
